32 devices in a mesh: group: 2 (over y), exp: 4 (over z), tok: 4 (over x, core).
Axes of the slice: x: 2, y: 2, z: 4, core: 2. Of those that a mesh axis runs over, the one named last changes fastest.
Arguments:
- activations: bfloat16 [1024, 2048], P(('group', 'exp'), 'tok'), parts along dimension 0, may hold values from -6 to 6
- expert_ids: int32 [1024, 4], P(('group', 'exp')), parts along dimension 0, may hold values from 0 to 7, all different within a row; in each aligned block of 128 rows (0 to 127, 128 to 255, ...) at most 128 rows name the same one
- gate_values: float32 [1024, 4], P(('group', 'exp')), parts along dimension 0, may hold values from 0.2 to 1
- expert_gate: bfloat16 [8, 2048, 512], P('exp', 'tok'), may hold values from -0.125 to 0.125
- expert_up: bfloat16 [8, 2048, 512], P('exp', 'tok'), may hold values from -0.125 to 0.125
- expert_down: bfloat16 [8, 512, 2048], P('exp', None, 'tok'), may hold values from -0.25 to 0.25
Outputs:
- layer_out: bfloat16 [1024, 2048], P(('group', 'exp'), 'tok'), parts along dimension 0
The draws below stay inside these ranges and needn't reach their ends.
There are 2 independent parts, one for each index of `group`. The reference program is written for one: setup_inputs(seed, part) draws one part's arguments, and reference() takes and returns one part's arrays. A program takes and returns all parts, laid end to end along the dimension named above; an argument that names none is the same for every part. Nothing has to cross between parts.
Inputs may be any that keep to these rules, and one draw needn't show every extreme that they name: `expert_ids`: each row names 4 different experts. Within each aligned block of 128 rows (the tokens of one index of exp) no expert is named by more than 128 rows, and in every draw some expert is named by exactly 128 rows of some block.
All inputs are finite; a program needn't handle non-finite values.
Results may differ from the reference program's by a relative error of at most 0.023.
Values may be sent and summed in bfloat16 or wider, within the bound.
A program may use at most 64 MiB of HBM per device.

```python
import math
import jax
import jax.numpy as jnp
import numpy as np
from jax import lax

D = 2048
FF = 512
TOP = 4
TOK_DEV = 128
EXPERTS = 8
CAP = 128
TOKENS = 512
N_EXP = 4
N_TOK = 4


def block_levels(stream_key, shape, shards, low, largest):
    gain, own = 1.0, jax.random.fold_in(stream_key, 6)
    for position, blocks in shards:
        steps = jnp.exp(jax.random.uniform(jax.random.fold_in(own, position), (blocks,), jnp.float32, low / len(shards), largest / len(shards)))
        gain = gain * jnp.repeat(steps, shape[position] // blocks).reshape([-1 if axis == position else 1 for axis in range(len(shape))])
    return gain


def assign_block(own_key, own, number, rows, amount, top, most, skew):
    sequence = jax.random.permutation(own_key, amount)
    heavy_load, usual = load_shares(amount, rows * top, most, skew, True), load_shares(amount, rows * top, most, skew, False)
    places = jnp.arange(amount)

    def named(sizes, offset_by):
        used = int((sizes > 0).sum())
        fixed = max(1, used // 4)
        shifted = fixed + (places - fixed + offset_by * (used - fixed)) % max(1, amount - fixed)
        return jnp.zeros((amount,), jnp.int32).at[sequence[jnp.where(places < fixed, places, shifted)]].set(jnp.asarray(sizes, jnp.int32))

    sizes = jnp.where(number % 4 == 0, named(heavy_load, number // 4), named(usual, number - number // 4 - 1))
    mixed = jax.random.permutation(jax.random.fold_in(own, 3), amount)
    donor, sink = mixed[0:amount // 2 * 2:2], mixed[1:amount // 2 * 2:2]
    slack = jnp.minimum(sizes[donor] - 1, most - sizes[sink]) // 2
    slack = jnp.where((donor == sequence[0]) | (sink == sequence[0]) | (sizes[sink] == 0), 0, jnp.maximum(slack, 0))
    shifted = jax.random.randint(jax.random.fold_in(own, 4), (amount // 2,), 0, 1 << 20) % (slack + 1)
    sizes = sizes.at[donor].add(-shifted).at[sink].add(shifted)
    items = jnp.searchsorted(jnp.cumsum(sizes), jnp.arange(rows * top), side="right").astype(jnp.int32)
    grid = items.reshape(top, rows).T
    grid = grid[jax.random.permutation(jax.random.fold_in(own, 1), rows)]
    offset_by = jax.random.randint(jax.random.fold_in(own, 2), (rows, 1), 0, top)
    return jnp.take_along_axis(grid, (jnp.arange(top)[None, :] + offset_by) % top, axis=1)


def load_shares(number_of, total, most, skew, full):
    portions = [(1 << 20) // math.isqrt(grade ** skew) + 1 for grade in range(1, number_of + 1)]
    largest = most if full else min(most, max(-(-total // number_of), total * portions[0] // sum(portions)))
    least = 1 if total - largest >= number_of - 1 else 0
    holding, spare = [largest] + [least] * (number_of - 1), total - largest - least * (number_of - 1)
    while spare > 0:
        free = [i for i in range(1, number_of) if holding[i] < largest] or [i for i in range(1, number_of) if holding[i] < most]
        pool, remaining = sum([portions[i] for i in free]), spare
        for i in free:
            extra = min(most - holding[i], max(1, remaining * portions[i] // pool), spare)
            holding[i] = holding[i] + extra
            spare = spare - extra
    return np.array(holding)


def gaussian(rng, extent, deviation, bound, cuts=(), kind=jnp.bfloat16):
    array = jax.random.normal(rng, extent, jnp.float32) * deviation
    if len(cuts) > 0:
        array = block_levels(rng, extent, cuts, -0.22, 0.18) * array
    return jnp.clip(array, min=-bound, max=bound).astype(kind)


def setup_inputs(seed: int = 0, part: int = 0) -> dict:
    key_list = jax.random.split(jax.random.key(seed), 7)
    part_splits = jax.random.split(jax.random.fold_in(key_list[6], part), 7)
    activations = gaussian(part_splits[0], (TOKENS, D), 1.0, 6.0, ((0, 4), (1, 4)))
    expert_ids_keys = jax.random.split(jax.random.fold_in(part_splits[1], 1), TOKENS // TOK_DEV)
    expert_ids_turns = jax.random.permutation(jax.random.fold_in(part_splits[1], 3), TOKENS // TOK_DEV)
    expert_ids = jax.vmap(lambda own, number: assign_block(jax.random.fold_in(part_splits[1], 2), own, number, TOK_DEV, EXPERTS, TOP, CAP, 2))(expert_ids_keys, expert_ids_turns).reshape((TOKENS, TOP))
    gate_values = jnp.clip(0.2 + 0.8 * jax.random.uniform(part_splits[2], (TOKENS, TOP), jnp.float32) ** block_levels(part_splits[2], (TOKENS, TOP), ((0, 4),), -0.2, 0.2), 0.2, 1.0)
    expert_gate = gaussian(key_list[3], (EXPERTS, D, FF), D ** -0.5, 0.125, ((0, 4), (1, 4)))
    expert_up = gaussian(key_list[4], (EXPERTS, D, FF), D ** -0.5, 0.125, ((0, 4), (1, 4)))
    expert_down = gaussian(key_list[5], (EXPERTS, FF, D), FF ** -0.5, 0.25, ((0, 4), (2, 4)))
    return {"activations": activations, "expert_ids": expert_ids, "gate_values": gate_values, "expert_gate": expert_gate, "expert_up": expert_up, "expert_down": expert_down}


def block_slots(block_ids):
    flat_ids = block_ids.reshape(-1).astype(jnp.int32)
    one_hot = (flat_ids[:, None] == jnp.arange(EXPERTS, dtype=jnp.int32)[None, :]).astype(jnp.int32)
    earlier = jnp.cumsum(one_hot, axis=0) - one_hot
    rank_within = jnp.sum(earlier * one_hot, axis=1)
    return (flat_ids * CAP + rank_within).astype(jnp.int32)


def slice_sum(rows, weights):
    sliced = rows.astype(jnp.float32).reshape(-1, N_TOK, D // N_TOK)
    parted = weights.astype(jnp.float32).reshape(N_TOK, D // N_TOK, FF)
    per_slice = jnp.einsum("rtf,tfh->trh", sliced, parted)
    rounded = lax.optimization_barrier(per_slice.astype(jnp.bfloat16))
    return jnp.sum(rounded.astype(jnp.float32), axis=0)


def expert_rows(inputs):
    rows, gate_w, up_w, down_w = inputs
    hidden = (jax.nn.silu(slice_sum(rows, gate_w)) * slice_sum(rows, up_w)).astype(jnp.bfloat16)
    return jnp.dot(hidden, down_w, preferred_element_type=jnp.float32).astype(jnp.bfloat16)


def reference(activations, expert_ids, gate_values, expert_gate, expert_up, expert_down):
    slots = jax.vmap(block_slots)(expert_ids.reshape(N_EXP, TOK_DEV, TOP))
    picked = jnp.repeat(activations, TOP, axis=0).reshape(N_EXP, TOK_DEV * TOP, D)
    sources = jnp.arange(N_EXP, dtype=jnp.int32)[:, None]
    buffer = jnp.zeros((N_EXP, EXPERTS * CAP, D), jnp.bfloat16).at[sources, slots].set(picked)
    by_expert = buffer.reshape(N_EXP, EXPERTS, CAP, D).transpose(1, 0, 2, 3).reshape(EXPERTS, N_EXP * CAP, D)
    outputs = lax.map(expert_rows, (by_expert, expert_gate, expert_up, expert_down))
    back = outputs.reshape(EXPERTS, N_EXP, CAP, D).transpose(1, 0, 2, 3).reshape(N_EXP, EXPERTS * CAP, D)
    fetched = jnp.take_along_axis(back, slots[:, :, None], axis=1).astype(jnp.float32)
    weighted = fetched.reshape(TOKENS, TOP, D) * gate_values[:, :, None]
    return jnp.sum(weighted, axis=1).astype(jnp.bfloat16)
```

```python
import functools

import jax
import jax.numpy as jnp
from jax import lax
from jax.experimental import pallas as pl
from jax.experimental.pallas import tpu as pltpu
from jax.sharding import PartitionSpec as P

MESH = pl.DeviceIdType.MESH


def slot_positions(expert_ids, experts_all, capacity):
    flat_ids = expert_ids.reshape(-1)
    one_hot = (flat_ids[:, None] == jnp.arange(experts_all, dtype=jnp.int32)[None, :]).astype(
        jnp.int32
    )
    earlier = jnp.cumsum(one_hot, axis=0) - one_hot
    rank_within = jnp.sum(earlier * one_hot, axis=1)
    return flat_ids * capacity + rank_within


def move_rows(buffer):
    return lax.all_to_all(buffer, "exp", split_axis=0, concat_axis=0, tiled=True)


def slot_layer(activations, expert_ids, gate_values, expert_gate, expert_up, expert_down):
    row_count, feature_cols = activations.shape
    top_count = expert_ids.shape[1]
    local_experts = expert_gate.shape[0]
    groups = lax.axis_size("exp")
    experts_all = local_experts * groups
    capacity = 2 * row_count * top_count // experts_all
    slot_index = slot_positions(expert_ids, experts_all, capacity)
    picked = jnp.repeat(activations, top_count, axis=0)
    outgoing = (
        jnp.zeros((experts_all * capacity, feature_cols), jnp.bfloat16).at[slot_index].set(picked)
    )
    arrived = move_rows(outgoing.reshape(groups, local_experts, capacity, feature_cols))
    gate_part = jnp.einsum(
        "sxcf,xfh->sxch", arrived, expert_gate, preferred_element_type=jnp.float32
    )
    up_part = jnp.einsum("sxcf,xfh->sxch", arrived, expert_up, preferred_element_type=jnp.float32)
    gate_pre, up_pre = (
        lax.psum(gate_part.astype(jnp.bfloat16), "tok").astype(jnp.float32),
        lax.psum(up_part.astype(jnp.bfloat16), "tok").astype(jnp.float32),
    )
    hidden = (jax.nn.silu(gate_pre) * up_pre).astype(jnp.bfloat16)
    results = jnp.einsum(
        "sxch,xhf->sxcf", hidden, expert_down, preferred_element_type=jnp.float32
    ).astype(jnp.bfloat16)
    returned = move_rows(results).reshape(experts_all * capacity, feature_cols)
    fetched = returned[slot_index].astype(jnp.float32).reshape(row_count, top_count, feature_cols)
    combined = jnp.sum(fetched * gate_values[:, :, None], axis=1)
    return combined.astype(jnp.bfloat16)


def block_order(n):
    return [sorted(range(n), key=lambda b: (abs(b - i), b)) for i in range(n)]


def skewed(n, stages):
    for tick in range(n + stages - 1):
        for stage in range(stages):
            if 0 <= tick - stage < n:
                yield stage, tick - stage


def dense_kernel(
    n, ids_ref, gv_ref, a_ref, wg_hbm, wu_hbm, wd_hbm, out_ref,
    wg, wu, wd, gates, xg, keep, csend, crecv, mine, xsend, xrecv, hid, outb, ret, acc,
    w_sem, z_send, z_recv, g_send, g_recv, c_send, c_recv, x_send, x_recv, h_send, h_recv,
    r_send, r_recv,
):
    rows = a_ref.shape[0]
    local_experts, _, ff = wg.shape
    half, quarter = rows // 2, rows // 4
    me, t = lax.axis_index("exp"), lax.axis_index("tok")
    c, xx = lax.rem(t, 2), lax.div(t, 2)
    core_peer, chip_peer = {"tok": xx * 2 + 1 - c}, {"tok": (1 - xx) * 2 + c}
    own_q, chip_q = c * 2 + xx, c * 2 + 1 - xx
    table = block_order(n)

    def block(step):
        b = me * 0
        for i in range(n):
            b = jnp.where(me == i, table[i][step], b)
        return b

    def send(src, dst, ss, rs, where):
        return pltpu.make_async_remote_copy(
            src_ref=src, dst_ref=dst, send_sem=ss, recv_sem=rs, device_id=where, device_id_type=MESH
        )

    weights = [
        pltpu.make_async_copy(src, dst, w_sem.at[i])
        for i, (src, dst) in enumerate(((wg_hbm, wg), (wu_hbm, wu), (wd_hbm, wd)))
    ]
    for copy in weights:
        copy.start()

    barrier = pltpu.get_barrier_semaphore()
    for j in range(1, n):
        pl.semaphore_signal(
            barrier, inc=1, device_id={"exp": lax.rem(me + j, n)}, device_id_type=MESH
        )
    for peer in (core_peer, chip_peer):
        pl.semaphore_signal(barrier, inc=1, device_id=peer, device_id_type=MESH)

    row0 = pl.multiple_of(own_q * quarter, quarter)
    ids, values = ids_ref[pl.ds(row0, quarter), :], gv_ref[pl.ds(row0, quarter), :]
    lanes = lax.broadcasted_iota(jnp.int32, gates.shape[1:], 1)
    table_of_gates = jnp.zeros(gates.shape[1:], jnp.float32)
    for k in range(ids.shape[1]):
        table_of_gates += jnp.where(lanes == ids[:, k : k + 1], values[:, k : k + 1], 0.0)
    gates[me] = table_of_gates
    pl.semaphore_wait(barrier, n + 1)

    def pass_on(b, src):
        return (
            (
                jnp.logical_and(b <= me, me < n - 1),
                send(src, xg.at[b], z_send.at[0, b], z_recv.at[b], {"exp": lax.rem(me + 1, n)}),
            ),
            (
                jnp.logical_and(b >= me, me > 0),
                send(src, xg.at[b], z_send.at[1, b], z_recv.at[b], {"exp": lax.rem(me + n - 1, n)}),
            ),
        )

    def start(copies):
        for condition, copy in copies:
            pl.when(condition)(copy.start)

    start(pass_on(me, a_ref))
    gate_copies = [
        send(gates.at[me], gates.at[me], g_send.at[j], g_recv.at[me], {"exp": lax.rem(me + j, n)})
        for j in range(1, n)
    ]
    for copy in gate_copies:
        copy.start()
    weights[0].wait()
    weights[1].wait()

    def to_core(s):
        return send(csend.at[s], crecv.at[s], c_send.at[s], c_recv.at[s], core_peer)

    def to_chip(s):
        return send(xsend.at[s], xrecv.at[s], x_send.at[s], x_recv.at[s], chip_peer)

    def hidden_copy(s, kind):
        q = (own_q, own_q, chip_q)[kind]
        peer = (chip_peer, core_peer, core_peer)[kind]
        return send(
            hid.at[s, q], hid.at[s, q], h_send.at[s, kind], h_recv.at[s, kind], peer
        )

    def hidden_arrival(s, kind):
        q = (chip_q, (1 - c) * 2 + xx, (1 - c) * 2 + 1 - xx)[kind]
        peer = (chip_peer, core_peer, core_peer)[kind]
        return send(
            hid.at[s, q], hid.at[s, q], h_send.at[s, kind], h_recv.at[s, kind], peer
        )

    def result_copy(s):
        b = block(s)
        return send(outb.at[s], ret.at[me], r_send.at[s], r_recv.at[me], {"exp": b})

    def partial(s):
        b = block(s)
        if s > 0:
            send(
                xg.at[b], xg.at[b], z_send.at[0, b], z_recv.at[b], {"exp": lax.rem(me + 1, n)}
            ).wait_recv()
            start(pass_on(b, xg.at[b]))
        first = pl.ds(pl.multiple_of(c * half, half), half)
        second = pl.ds(pl.multiple_of((1 - c) * half, half), half)
        if s == 0:
            block_rows = jnp.concatenate([a_ref[first, :], a_ref[second, :]], axis=0)
        else:
            block_rows = jnp.concatenate([xg[b, first, :], xg[b, second, :]], axis=0)
        for e in range(local_experts):
            for i, w in enumerate((wg, wu)):
                part = jnp.dot(block_rows, w[e], preferred_element_type=jnp.float32)
                cols = pl.ds((2 * e + i) * ff, ff)
                csend[s, :, cols] = part[half:].astype(jnp.bfloat16)
                keep[s, :, cols] = part[:half]
        to_core(s).start()

    def chip_sum(s):
        to_core(s).wait_recv()
        own = pl.ds(pl.multiple_of(xx * quarter, quarter), quarter)
        other = pl.ds(pl.multiple_of((1 - xx) * quarter, quarter), quarter)
        xsend[s] = (keep[s, other, :] + crecv[s, other, :].astype(jnp.float32)).astype(jnp.bfloat16)
        to_chip(s).start()
        mine[s] = keep[s, own, :] + crecv[s, own, :].astype(jnp.float32)

    def activate(s):
        b = block(s)
        if s > 0:
            send(
                gates.at[b], gates.at[b], g_send.at[s], g_recv.at[b], {"exp": lax.rem(me + 1, n)}
            ).wait_recv()
        to_chip(s).wait_recv()
        weight_of = gates[b]
        for e in range(local_experts):
            gate_cols, up_cols = pl.ds(2 * e * ff, ff), pl.ds((2 * e + 1) * ff, ff)
            g = mine[s, :, gate_cols] + xrecv[s, :, gate_cols].astype(jnp.float32)
            u = mine[s, :, up_cols] + xrecv[s, :, up_cols].astype(jnp.float32)
            scale = jnp.sum(
                jnp.where(lanes == me * local_experts + e, weight_of, 0.0), axis=1, keepdims=True
            )
            hid[s, own_q, :, pl.ds(e * ff, ff)] = (g / (1.0 + jnp.exp(-g)) * (u * scale)).astype(
                jnp.bfloat16
            )
        hidden_copy(s, 0).start()
        hidden_copy(s, 1).start()

    def hand_on(s):
        hidden_arrival(s, 0).wait_recv()
        hidden_copy(s, 2).start()

    def project(s):
        hidden_arrival(s, 1).wait_recv()
        hidden_arrival(s, 2).wait_recv()
        if s == 0:
            weights[2].wait()
        h = hid[s].reshape(rows, local_experts * ff)
        result = jnp.dot(
            h, wd[...].reshape(local_experts * ff, wd.shape[2]), preferred_element_type=jnp.float32
        )
        if s == 0:
            acc[...] = result
        else:
            outb[s] = result.astype(jnp.bfloat16)
            result_copy(s).start()

    stages = (partial, chip_sum, activate, hand_on, project)
    for stage, s in skewed(n, len(stages)):
        stages[stage](s)

    total = acc[...]
    for s in range(1, n):
        b = block(s)
        send(
            outb.at[s], ret.at[b], r_send.at[s], r_recv.at[b], {"exp": b}
        ).wait_recv()
        total += ret[b].astype(jnp.float32)
    out_ref[...] = total.astype(out_ref.dtype)

    for s in range(n):
        b = block(s)
        for condition, copy in pass_on(b, a_ref if s == 0 else xg.at[b]):
            pl.when(condition)(copy.wait_send)
        to_core(s).wait_send()
        to_chip(s).wait_send()
        for kind in range(3):
            hidden_copy(s, kind).wait_send()
        if s > 0:
            result_copy(s).wait_send()
    for copy in gate_copies:
        copy.wait_send()


def dense_layer(activations, expert_ids, gate_values, expert_gate, expert_up, expert_down):
    n = lax.axis_size("exp")
    rows, cols = activations.shape
    local_experts, _, ff = expert_gate.shape
    wide, joined = 2 * local_experts * ff, local_experts * ff
    half, quarter = rows // 2, rows // 4
    lanes = -(-local_experts * n // 128) * 128
    bf16, f32 = jnp.bfloat16, jnp.float32
    vmem, hbm = pl.BlockSpec(memory_space=pltpu.VMEM), pl.BlockSpec(memory_space=pl.ANY)
    dma = pltpu.SemaphoreType.DMA
    return pl.pallas_call(
        functools.partial(dense_kernel, n),
        out_shape=jax.ShapeDtypeStruct((rows, cols), bf16),
        in_specs=[vmem, vmem, vmem, hbm, hbm, hbm],
        out_specs=vmem,
        scratch_shapes=[
            pltpu.VMEM(expert_gate.shape, bf16),
            pltpu.VMEM(expert_up.shape, bf16),
            pltpu.VMEM(expert_down.shape, bf16),
            pltpu.VMEM((n, quarter, lanes), f32),
            pltpu.VMEM((n, rows, cols), bf16),
            pltpu.VMEM((n, half, wide), f32),
            pltpu.VMEM((n, half, wide), bf16),
            pltpu.VMEM((n, half, wide), bf16),
            pltpu.VMEM((n, quarter, wide), f32),
            pltpu.VMEM((n, quarter, wide), bf16),
            pltpu.VMEM((n, quarter, wide), bf16),
            pltpu.VMEM((n, 4, quarter, joined), bf16),
            pltpu.VMEM((n, rows, cols), bf16),
            pltpu.VMEM((n, rows, cols), bf16),
            pltpu.VMEM((rows, cols), f32),
            dma((3,)),
            dma((2, n)),
            dma((n,)),
            dma((n,)),
            dma((n,)),
            dma((n,)),
            dma((n,)),
            dma((n,)),
            dma((n,)),
            dma((n, 3)),
            dma((n, 3)),
            dma((n,)),
            dma((n,)),
        ],
        compiler_params=pltpu.CompilerParams(
            collective_id=0, has_side_effects=True, vmem_limit_bytes=48 * 1024 * 1024
        ),
    )(expert_ids, gate_values, activations, expert_gate, expert_up, expert_down)


def shards(activations, expert_ids, gate_values, expert_gate, expert_up, expert_down):
    rows = activations.shape[0]
    experts_all = expert_gate.shape[0] * lax.axis_size("exp")
    capacity = 2 * rows * expert_ids.shape[1] // experts_all
    layer = dense_layer if capacity >= rows and lax.axis_size("tok") == 4 else slot_layer
    return layer(activations, expert_ids, gate_values, expert_gate, expert_up, expert_down)


def solution(mesh):
    placed = (
        P(("group", "exp"), "tok"),
        P(("group", "exp"), None),
        P(("group", "exp"), None),
        P("exp", "tok", None),
        P("exp", "tok", None),
        P("exp", None, "tok"),
    )
    return jax.shard_map(
        shards, mesh=mesh, in_specs=placed, out_specs=P(("group", "exp"), "tok"), check_vma=False
    )
```

```python
import functools

import jax
import jax.numpy as jnp
from jax import lax
from jax.experimental import pallas as pl
from jax.experimental.pallas import tpu as pltpu
from jax.sharding import PartitionSpec as P

MESH = pl.DeviceIdType.MESH


def slot_positions(expert_ids, experts_all, capacity):
    flat_ids = expert_ids.reshape(-1)
    one_hot = (flat_ids[:, None] == jnp.arange(experts_all, dtype=jnp.int32)[None, :]).astype(
        jnp.int32
    )
    earlier = jnp.cumsum(one_hot, axis=0) - one_hot
    rank_within = jnp.sum(earlier * one_hot, axis=1)
    return flat_ids * capacity + rank_within


def move_rows(buffer):
    return lax.all_to_all(buffer, "exp", split_axis=0, concat_axis=0, tiled=True)


def slot_layer(activations, expert_ids, gate_values, expert_gate, expert_up, expert_down):
    row_count, feature_cols = activations.shape
    top_count = expert_ids.shape[1]
    local_experts = expert_gate.shape[0]
    groups = lax.axis_size("exp")
    experts_all = local_experts * groups
    capacity = 2 * row_count * top_count // experts_all
    slot_index = slot_positions(expert_ids, experts_all, capacity)
    picked = jnp.repeat(activations, top_count, axis=0)
    outgoing = (
        jnp.zeros((experts_all * capacity, feature_cols), jnp.bfloat16).at[slot_index].set(picked)
    )
    arrived = move_rows(outgoing.reshape(groups, local_experts, capacity, feature_cols))
    gate_part = jnp.einsum(
        "sxcf,xfh->sxch", arrived, expert_gate, preferred_element_type=jnp.float32
    )
    up_part = jnp.einsum("sxcf,xfh->sxch", arrived, expert_up, preferred_element_type=jnp.float32)
    gate_pre, up_pre = (
        lax.psum(gate_part.astype(jnp.bfloat16), "tok").astype(jnp.float32),
        lax.psum(up_part.astype(jnp.bfloat16), "tok").astype(jnp.float32),
    )
    hidden = (jax.nn.silu(gate_pre) * up_pre).astype(jnp.bfloat16)
    results = jnp.einsum(
        "sxch,xhf->sxcf", hidden, expert_down, preferred_element_type=jnp.float32
    ).astype(jnp.bfloat16)
    returned = move_rows(results).reshape(experts_all * capacity, feature_cols)
    fetched = returned[slot_index].astype(jnp.float32).reshape(row_count, top_count, feature_cols)
    combined = jnp.sum(fetched * gate_values[:, :, None], axis=1)
    return combined.astype(jnp.bfloat16)


def block_order(n):
    return [sorted(range(n), key=lambda b: (abs(b - i), b)) for i in range(n)]


def run_order(n):
    if n < 4:
        return [(k, s) for k in "ABCDE" for s in range(n) if (k, s) != ("A", 0)]
    last, middle = n - 1, range(1, n - 2)
    plan = [("B", 0)]
    plan += [(k, s) for s in range(1, last) for k in "AB"]
    plan += [("C", s) for s in range(n - 2)]
    plan += [("A", last), ("B", last)]
    plan += [("D", s) for s in middle] + [("C", n - 2), ("D", 0)] + [("E", s) for s in middle]
    plan += [("C", last), ("D", n - 2), ("E", n - 2), ("E", 0), ("D", last), ("E", last)]
    return plan


def dense_kernel(
    n, ids_hbm, gv_hbm, a_hbm, wg_hbm, wu_hbm, wd_hbm, out_ref,
    ids_ref, gv_ref, wg, wu, wd, gates, xg, keep, csend, crecv, mine, xsend, xrecv, hid, outb, ret, acc,
    w_sem, z_send, z_recv, g_send, g_recv, c_send, c_recv, x_send, x_recv, h_send, h_recv,
    r_send, r_recv,
):
    rows = xg.shape[1]
    local_experts, _, ff = wg.shape
    half, quarter = rows // 2, rows // 4
    me, t = lax.axis_index("exp"), lax.axis_index("tok")
    c, xx = lax.rem(t, 2), lax.div(t, 2)
    core_peer, chip_peer = {"tok": xx * 2 + 1 - c}, {"tok": (1 - xx) * 2 + c}
    own_q, chip_q = c * 2 + xx, c * 2 + 1 - xx
    table = block_order(n)

    def block(step):
        b = me * 0
        for i in range(n):
            b = jnp.where(me == i, table[i][step], b)
        return b

    def send(src, dst, ss, rs, where):
        return pltpu.make_async_remote_copy(
            src_ref=src, dst_ref=dst, send_sem=ss, recv_sem=rs, device_id=where, device_id_type=MESH
        )

    loads = [
        pltpu.make_async_copy(src, dst, w_sem.at[i])
        for i, (src, dst) in enumerate(
            (
                (a_hbm, xg.at[me]),
                (wg_hbm, wg),
                (wu_hbm, wu),
                (ids_hbm, ids_ref),
                (gv_hbm, gv_ref),
                (wd_hbm, wd),
            )
        )
    ]
    for copy in loads:
        copy.start()

    barrier = pltpu.get_barrier_semaphore()
    for j in range(1, n):
        pl.semaphore_signal(
            barrier, inc=1, device_id={"exp": lax.rem(me + j, n)}, device_id_type=MESH
        )
    for peer in (core_peer, chip_peer):
        pl.semaphore_signal(barrier, inc=1, device_id=peer, device_id_type=MESH)

    def spread(buffer, send_sem, recv_sem):
        return [
            (
                jnp.logical_and(peer >= 0, peer < n),
                send(
                    buffer.at[me], buffer.at[me], send_sem.at[i], recv_sem.at[me],
                    {"exp": jnp.clip(peer, 0, n - 1)},
                ),
            )
            for i, peer in enumerate(me + d * sign for d in range(1, n) for sign in (1, -1))
        ]

    row_copies, gate_copies = spread(xg, z_send, z_recv), spread(gates, g_send, g_recv)

    def to_core(s):
        return send(csend.at[s], crecv.at[s], c_send.at[s], c_recv.at[s], core_peer)

    def to_chip(s):
        return send(xsend.at[s], xrecv.at[s], x_send.at[s], x_recv.at[s], chip_peer)

    def hidden_copy(s, kind):
        q = (own_q, own_q, chip_q)[kind]
        peer = (chip_peer, core_peer, core_peer)[kind]
        return send(
            hid.at[s, q], hid.at[s, q], h_send.at[s, kind], h_recv.at[s, kind], peer
        )

    def hidden_arrival(s, kind):
        q = (chip_q, (1 - c) * 2 + xx, (1 - c) * 2 + 1 - xx)[kind]
        peer = (chip_peer, core_peer, core_peer)[kind]
        return send(
            hid.at[s, q], hid.at[s, q], h_send.at[s, kind], h_recv.at[s, kind], peer
        )

    def result_copy(s):
        b = block(s)
        return send(outb.at[s], ret.at[me], r_send.at[s], r_recv.at[me], {"exp": b})

    def partial(s):
        b = block(s)
        if s > 0:
            send(
                xg.at[b], xg.at[b], z_send.at[0], z_recv.at[b], {"exp": lax.rem(me + 1, n)}
            ).wait_recv()
        first = pl.ds(pl.multiple_of(c * half, half), half)
        second = pl.ds(pl.multiple_of((1 - c) * half, half), half)
        block_rows = jnp.concatenate([xg[b, first, :], xg[b, second, :]], axis=0)
        for e in range(local_experts):
            for i, w in enumerate((wg, wu)):
                part = jnp.dot(block_rows, w[e], preferred_element_type=jnp.float32)
                cols = pl.ds((2 * e + i) * ff, ff)
                csend[s, :, cols] = part[half:].astype(jnp.bfloat16)
                keep[s, :, cols] = part[:half]
        if s > 0:
            to_core(s).start()

    def chip_sum(s):
        to_core(s).wait_recv()
        own = pl.ds(pl.multiple_of(xx * quarter, quarter), quarter)
        other = pl.ds(pl.multiple_of((1 - xx) * quarter, quarter), quarter)
        xsend[s] = (keep[s, other, :] + crecv[s, other, :].astype(jnp.float32)).astype(jnp.bfloat16)
        to_chip(s).start()
        mine[s] = keep[s, own, :] + crecv[s, own, :].astype(jnp.float32)

    def activate(s):
        b = block(s)
        if s > 0:
            send(
                gates.at[b], gates.at[b], g_send.at[0], g_recv.at[b], {"exp": lax.rem(me + 1, n)}
            ).wait_recv()
        to_chip(s).wait_recv()
        square = (quarter, rows)
        diagonal = lax.broadcasted_iota(jnp.int32, square, 1) == (
            own_q * quarter + lax.broadcasted_iota(jnp.int32, square, 0)
        )
        for e in range(local_experts):
            gate_cols, up_cols = pl.ds(2 * e * ff, ff), pl.ds((2 * e + 1) * ff, ff)
            g = mine[s, :, gate_cols] + xrecv[s, :, gate_cols].astype(jnp.float32)
            u = mine[s, :, up_cols] + xrecv[s, :, up_cols].astype(jnp.float32)
            weight_of = gates[b, pl.ds(me * local_experts + e, 1), :]
            scale = jnp.sum(jnp.where(diagonal, weight_of, 0.0), axis=1, keepdims=True)
            hid[s, own_q, :, pl.ds(e * ff, ff)] = (g / (1.0 + jnp.exp(-g)) * (u * scale)).astype(
                jnp.bfloat16
            )
        hidden_copy(s, 0).start()
        hidden_copy(s, 1).start()

    def hand_on(s):
        hidden_arrival(s, 0).wait_recv()
        hidden_copy(s, 2).start()

    def project(s):
        hidden_arrival(s, 1).wait_recv()
        hidden_arrival(s, 2).wait_recv()
        if s == first_projected:
            loads[5].wait()
        h = hid[s].reshape(rows, local_experts * ff)
        result = jnp.dot(
            h, wd[...].reshape(local_experts * ff, wd.shape[2]), preferred_element_type=jnp.float32
        )
        if s == 0:
            acc[...] = result
        else:
            outb[s] = result.astype(jnp.bfloat16)
            result_copy(s).start()

    stages = {"A": partial, "B": chip_sum, "C": activate, "D": hand_on, "E": project}
    plan = run_order(n)
    first_projected = next(s for stage, s in plan if stage == "E")

    for copy in loads[:3]:
        copy.wait()
    partial(0)
    for copy in loads[3:5]:
        copy.wait()
    experts = lax.broadcasted_iota(jnp.int32, gates.shape[1:], 0)
    table_of_gates = jnp.zeros(gates.shape[1:], jnp.float32)
    for k in range(ids_ref.shape[0]):
        table_of_gates += jnp.where(experts == ids_ref[k : k + 1, :], gv_ref[k : k + 1, :], 0.0)
    gates[me] = table_of_gates
    pl.semaphore_wait(barrier, n + 1)
    to_core(0).start()
    for condition, copy in row_copies + gate_copies:
        pl.when(condition)(copy.start)
    for stage, s in plan:
        stages[stage](s)

    total = acc[...]
    for s in range(1, n):
        b = block(s)
        send(
            outb.at[s], ret.at[b], r_send.at[s], r_recv.at[b], {"exp": b}
        ).wait_recv()
        total += ret[b].astype(jnp.float32)
    out_ref[...] = total.astype(out_ref.dtype)

    for s in range(n):
        to_core(s).wait_send()
        to_chip(s).wait_send()
        for kind in range(3):
            hidden_copy(s, kind).wait_send()
        if s > 0:
            result_copy(s).wait_send()
    for condition, copy in row_copies + gate_copies:
        pl.when(condition)(copy.wait_send)


def dense_layer(activations, expert_ids, gate_values, expert_gate, expert_up, expert_down):
    n = lax.axis_size("exp")
    rows, cols = activations.shape
    local_experts, _, ff = expert_gate.shape
    wide, joined = 2 * local_experts * ff, local_experts * ff
    half, quarter = rows // 2, rows // 4
    experts = -(-local_experts * n // 8) * 8
    top = expert_ids.shape[1]
    bf16, f32 = jnp.bfloat16, jnp.float32
    vmem, hbm = pl.BlockSpec(memory_space=pltpu.VMEM), pl.BlockSpec(memory_space=pltpu.HBM)
    dma = pltpu.SemaphoreType.DMA
    return pl.pallas_call(
        functools.partial(dense_kernel, n),
        out_shape=jax.ShapeDtypeStruct((rows, cols), bf16),
        in_specs=[hbm] * 6,
        out_specs=vmem,
        scratch_shapes=[
            pltpu.VMEM((top, rows), jnp.int32),
            pltpu.VMEM((top, rows), f32),
            pltpu.VMEM(expert_gate.shape, bf16),
            pltpu.VMEM(expert_up.shape, bf16),
            pltpu.VMEM(expert_down.shape, bf16),
            pltpu.VMEM((n, experts, rows), f32),
            pltpu.VMEM((n, rows, cols), bf16),
            pltpu.VMEM((n, half, wide), f32),
            pltpu.VMEM((n, half, wide), bf16),
            pltpu.VMEM((n, half, wide), bf16),
            pltpu.VMEM((n, quarter, wide), f32),
            pltpu.VMEM((n, quarter, wide), bf16),
            pltpu.VMEM((n, quarter, wide), bf16),
            pltpu.VMEM((n, 4, quarter, joined), bf16),
            pltpu.VMEM((n, rows, cols), bf16),
            pltpu.VMEM((n, rows, cols), bf16),
            pltpu.VMEM((rows, cols), f32),
            dma((6,)),
            dma((2 * n - 2,)),
            dma((n,)),
            dma((2 * n - 2,)),
            dma((n,)),
            dma((n,)),
            dma((n,)),
            dma((n,)),
            dma((n,)),
            dma((n, 3)),
            dma((n, 3)),
            dma((n,)),
            dma((n,)),
        ],
        compiler_params=pltpu.CompilerParams(
            collective_id=0, has_side_effects=True, vmem_limit_bytes=67043328
        ),
    )(expert_ids.T, gate_values.T, activations, expert_gate, expert_up, expert_down)


def shards(activations, expert_ids, gate_values, expert_gate, expert_up, expert_down):
    rows = activations.shape[0]
    experts_all = expert_gate.shape[0] * lax.axis_size("exp")
    capacity = 2 * rows * expert_ids.shape[1] // experts_all
    layer = dense_layer if capacity >= rows and lax.axis_size("tok") == 4 else slot_layer
    return layer(activations, expert_ids, gate_values, expert_gate, expert_up, expert_down)


def solution(mesh):
    placed = (
        P(("group", "exp"), "tok"),
        P(("group", "exp"), None),
        P(("group", "exp"), None),
        P("exp", "tok", None),
        P("exp", "tok", None),
        P("exp", None, "tok"),
    )
    return jax.shard_map(
        shards, mesh=mesh, in_specs=placed, out_specs=P(("group", "exp"), "tok"), check_vma=False
    )
```

```python
import functools

import jax
import jax.numpy as jnp
from jax import lax
from jax.experimental import pallas as pl
from jax.experimental.pallas import tpu as pltpu
from jax.sharding import PartitionSpec as P

MESH = pl.DeviceIdType.MESH


def slot_positions(expert_ids, experts_all, capacity):
    flat_ids = expert_ids.reshape(-1)
    one_hot = (flat_ids[:, None] == jnp.arange(experts_all, dtype=jnp.int32)[None, :]).astype(
        jnp.int32
    )
    earlier = jnp.cumsum(one_hot, axis=0) - one_hot
    rank_within = jnp.sum(earlier * one_hot, axis=1)
    return flat_ids * capacity + rank_within


def move_rows(buffer):
    return lax.all_to_all(buffer, "exp", split_axis=0, concat_axis=0, tiled=True)


def slot_layer(activations, expert_ids, gate_values, expert_gate, expert_up, expert_down):
    row_count, feature_cols = activations.shape
    top_count = expert_ids.shape[1]
    local_experts = expert_gate.shape[0]
    groups = lax.axis_size("exp")
    experts_all = local_experts * groups
    capacity = 2 * row_count * top_count // experts_all
    slot_index = slot_positions(expert_ids, experts_all, capacity)
    picked = jnp.repeat(activations, top_count, axis=0)
    outgoing = (
        jnp.zeros((experts_all * capacity, feature_cols), jnp.bfloat16).at[slot_index].set(picked)
    )
    arrived = move_rows(outgoing.reshape(groups, local_experts, capacity, feature_cols))
    gate_part = jnp.einsum(
        "sxcf,xfh->sxch", arrived, expert_gate, preferred_element_type=jnp.float32
    )
    up_part = jnp.einsum("sxcf,xfh->sxch", arrived, expert_up, preferred_element_type=jnp.float32)
    gate_pre, up_pre = (
        lax.psum(gate_part.astype(jnp.bfloat16), "tok").astype(jnp.float32),
        lax.psum(up_part.astype(jnp.bfloat16), "tok").astype(jnp.float32),
    )
    hidden = (jax.nn.silu(gate_pre) * up_pre).astype(jnp.bfloat16)
    results = jnp.einsum(
        "sxch,xhf->sxcf", hidden, expert_down, preferred_element_type=jnp.float32
    ).astype(jnp.bfloat16)
    returned = move_rows(results).reshape(experts_all * capacity, feature_cols)
    fetched = returned[slot_index].astype(jnp.float32).reshape(row_count, top_count, feature_cols)
    combined = jnp.sum(fetched * gate_values[:, :, None], axis=1)
    return combined.astype(jnp.bfloat16)


def block_order(n):
    return [sorted(range(n), key=lambda b: (abs(b - i), b)) for i in range(n)]


def run_order(n):
    if n < 4:
        return [(k, s) for k in "FABCDE" for s in range(n) if s > 0 or k not in "FA"]
    last, middle = n - 1, range(1, n - 2)
    plan = [("B", 0), ("F", 1)]
    plan += [(k, s) for s in range(1, last) for k in ("FAB" if s > 1 else "AB")]
    plan += [("C", 0), ("F", last)] + [("C", s) for s in middle]
    plan += [("A", last), ("B", last)]
    plan += [("D", s) for s in middle] + [("C", n - 2), ("D", 0)] + [("E", s) for s in middle]
    plan += [("C", last), ("D", n - 2), ("E", n - 2), ("E", 0), ("D", last), ("E", last)]
    return plan


def dense_kernel(
    n, ids_hbm, gv_hbm, a_hbm, wg_hbm, wu_hbm, wd_hbm, out_ref,
    ids_ref, gv_ref, wg, wu, wd, gates, xg, keep, csend, crecv, mine, xsend, xrecv, hid, outb, ret, acc,
    w_sem, z_send, z_recv, g_send, g_recv, c_send, c_recv, x_send, x_recv, h_send, h_recv,
    r_send, r_recv,
):
    rows = xg.shape[1]
    local_experts, _, ff = wg.shape
    half, quarter = rows // 2, rows // 4
    me, t = lax.axis_index("exp"), lax.axis_index("tok")
    c, xx = lax.rem(t, 2), lax.div(t, 2)
    core_peer, chip_peer = {"tok": xx * 2 + 1 - c}, {"tok": (1 - xx) * 2 + c}
    own_q, chip_q = c * 2 + xx, c * 2 + 1 - xx
    table = block_order(n)

    def block(step):
        b = me * 0
        for i in range(n):
            b = jnp.where(me == i, table[i][step], b)
        return b

    def send(src, dst, ss, rs, where):
        return pltpu.make_async_remote_copy(
            src_ref=src, dst_ref=dst, send_sem=ss, recv_sem=rs, device_id=where, device_id_type=MESH
        )

    loads = [
        pltpu.make_async_copy(src, dst, w_sem.at[i])
        for i, (src, dst) in enumerate(
            (
                (a_hbm, xg.at[me]),
                (ids_hbm, ids_ref),
                (gv_hbm, gv_ref),
                (wg_hbm, wg),
                (wu_hbm, wu),
                (wd_hbm, wd),
            )
        )
    ]
    for copy in loads:
        copy.start()

    barrier = pltpu.get_barrier_semaphore()
    for j in range(1, n):
        pl.semaphore_signal(
            barrier, inc=1, device_id={"exp": lax.rem(me + j, n)}, device_id_type=MESH
        )
    for peer in (core_peer, chip_peer):
        pl.semaphore_signal(barrier, inc=1, device_id=peer, device_id_type=MESH)

    def spread(buffer, send_sem, recv_sem):
        return [
            (
                jnp.logical_and(peer >= 0, peer < n),
                send(
                    buffer.at[me], buffer.at[me], send_sem.at[i], recv_sem.at[me],
                    {"exp": jnp.clip(peer, 0, n - 1)},
                ),
            )
            for i, peer in enumerate(me + d * sign for d in range(1, n) for sign in (1, -1))
        ]

    gate_copies = spread(gates, g_send, g_recv)
    inner = jnp.logical_and(me > 0, me < n - 1)
    row_copies = [
        (
            jnp.logical_and(peer >= 0, peer < n),
            send(xg.at[me], xg.at[me], z_send.at[0, i], z_recv.at[me], {"exp": lax.rem(peer + n, n)}),
        )
        for i, peer in enumerate((me + 1, me - 1))
    ]

    def onward(s):
        b = block(s)
        peer = jnp.where(b < me, me + 1, me - 1)
        return send(
            xg.at[b], xg.at[b], z_send.at[1, s], z_recv.at[b], {"exp": lax.rem(peer + n, n)}
        )

    def hand_rows(s):
        @pl.when(inner)
        def _():
            onward(s).wait_recv()
            onward(s).start()

    def to_core(s):
        return send(csend.at[s], crecv.at[s], c_send.at[s], c_recv.at[s], core_peer)

    def to_chip(s):
        return send(xsend.at[s], xrecv.at[s], x_send.at[s], x_recv.at[s], chip_peer)

    def hidden_copy(s, kind):
        q = (own_q, own_q, chip_q)[kind]
        peer = (chip_peer, core_peer, core_peer)[kind]
        return send(
            hid.at[s, q], hid.at[s, q], h_send.at[s, kind], h_recv.at[s, kind], peer
        )

    def hidden_arrival(s, kind):
        q = (chip_q, (1 - c) * 2 + xx, (1 - c) * 2 + 1 - xx)[kind]
        peer = (chip_peer, core_peer, core_peer)[kind]
        return send(
            hid.at[s, q], hid.at[s, q], h_send.at[s, kind], h_recv.at[s, kind], peer
        )

    def result_copy(s):
        b = block(s)
        return send(outb.at[s], ret.at[me], r_send.at[s], r_recv.at[me], {"exp": b})

    def partial(s):
        b = block(s)
        if s > 0:
            pl.when(jnp.logical_not(inner))(onward(s).wait_recv)
        first = pl.ds(pl.multiple_of(c * half, half), half)
        second = pl.ds(pl.multiple_of((1 - c) * half, half), half)
        block_rows = jnp.concatenate([xg[b, first, :], xg[b, second, :]], axis=0)
        for e in range(local_experts):
            for i, w in enumerate((wg, wu)):
                part = jnp.dot(block_rows, w[e], preferred_element_type=jnp.float32)
                cols = pl.ds((2 * e + i) * ff, ff)
                csend[s, :, cols] = part[half:].astype(jnp.bfloat16)
                keep[s, :, cols] = part[:half]
        to_core(s).start()

    def chip_sum(s):
        to_core(s).wait_recv()
        own = pl.ds(pl.multiple_of(xx * quarter, quarter), quarter)
        other = pl.ds(pl.multiple_of((1 - xx) * quarter, quarter), quarter)
        xsend[s] = (keep[s, other, :] + crecv[s, other, :].astype(jnp.float32)).astype(jnp.bfloat16)
        to_chip(s).start()
        mine[s] = keep[s, own, :] + crecv[s, own, :].astype(jnp.float32)

    def activate(s):
        b = block(s)
        if s > 0:
            send(
                gates.at[b], gates.at[b], g_send.at[0], g_recv.at[b], {"exp": lax.rem(me + 1, n)}
            ).wait_recv()
        to_chip(s).wait_recv()
        square = (quarter, rows)
        diagonal = lax.broadcasted_iota(jnp.int32, square, 1) == (
            own_q * quarter + lax.broadcasted_iota(jnp.int32, square, 0)
        )
        for e in range(local_experts):
            gate_cols, up_cols = pl.ds(2 * e * ff, ff), pl.ds((2 * e + 1) * ff, ff)
            g = mine[s, :, gate_cols] + xrecv[s, :, gate_cols].astype(jnp.float32)
            u = mine[s, :, up_cols] + xrecv[s, :, up_cols].astype(jnp.float32)
            weight_of = gates[b, pl.ds(me * local_experts + e, 1), :]
            scale = jnp.sum(jnp.where(diagonal, weight_of, 0.0), axis=1, keepdims=True)
            hid[s, own_q, :, pl.ds(e * ff, ff)] = (g / (1.0 + jnp.exp(-g)) * (u * scale)).astype(
                jnp.bfloat16
            )
        hidden_copy(s, 0).start()
        hidden_copy(s, 1).start()

    def hand_on(s):
        hidden_arrival(s, 0).wait_recv()
        hidden_copy(s, 2).start()

    def project(s):
        hidden_arrival(s, 1).wait_recv()
        hidden_arrival(s, 2).wait_recv()
        if s == first_projected:
            loads[5].wait()
        h = hid[s].reshape(rows, local_experts * ff)
        result = jnp.dot(
            h, wd[...].reshape(local_experts * ff, wd.shape[2]), preferred_element_type=jnp.float32
        )
        if s == 0:
            acc[...] = result
        else:
            outb[s] = result.astype(jnp.bfloat16)
            result_copy(s).start()

    stages = {"A": partial, "B": chip_sum, "C": activate, "D": hand_on, "E": project, "F": hand_rows}
    plan = run_order(n)
    first_projected = next(s for stage, s in plan if stage == "E")

    for copy in loads[:3]:
        copy.wait()
    experts = lax.broadcasted_iota(jnp.int32, gates.shape[1:], 0)
    table_of_gates = jnp.zeros(gates.shape[1:], jnp.float32)
    for k in range(ids_ref.shape[0]):
        table_of_gates += jnp.where(experts == ids_ref[k : k + 1, :], gv_ref[k : k + 1, :], 0.0)
    gates[me] = table_of_gates
    pl.semaphore_wait(barrier, n + 1)
    for condition, copy in row_copies + gate_copies:
        pl.when(condition)(copy.start)
    for copy in loads[3:5]:
        copy.wait()
    partial(0)
    for stage, s in plan:
        stages[stage](s)

    total = acc[...]
    for s in range(1, n):
        b = block(s)
        send(
            outb.at[s], ret.at[b], r_send.at[s], r_recv.at[b], {"exp": b}
        ).wait_recv()
        total += ret[b].astype(jnp.float32)
    out_ref[...] = total.astype(out_ref.dtype)

    for s in range(n):
        to_core(s).wait_send()
        to_chip(s).wait_send()
        for kind in range(3):
            hidden_copy(s, kind).wait_send()
        if s > 0:
            result_copy(s).wait_send()
    for condition, copy in row_copies + gate_copies:
        pl.when(condition)(copy.wait_send)
    for s in range(1, n):
        pl.when(inner)(onward(s).wait_send)


def dense_layer(activations, expert_ids, gate_values, expert_gate, expert_up, expert_down):
    n = lax.axis_size("exp")
    rows, cols = activations.shape
    local_experts, _, ff = expert_gate.shape
    wide, joined = 2 * local_experts * ff, local_experts * ff
    half, quarter = rows // 2, rows // 4
    experts = -(-local_experts * n // 8) * 8
    top = expert_ids.shape[1]
    bf16, f32 = jnp.bfloat16, jnp.float32
    vmem, hbm = pl.BlockSpec(memory_space=pltpu.VMEM), pl.BlockSpec(memory_space=pltpu.HBM)
    dma = pltpu.SemaphoreType.DMA
    return pl.pallas_call(
        functools.partial(dense_kernel, n),
        out_shape=jax.ShapeDtypeStruct((rows, cols), bf16),
        in_specs=[hbm] * 6,
        out_specs=vmem,
        scratch_shapes=[
            pltpu.VMEM((top, rows), jnp.int32),
            pltpu.VMEM((top, rows), f32),
            pltpu.VMEM(expert_gate.shape, bf16),
            pltpu.VMEM(expert_up.shape, bf16),
            pltpu.VMEM(expert_down.shape, bf16),
            pltpu.VMEM((n, experts, rows), f32),
            pltpu.VMEM((n, rows, cols), bf16),
            pltpu.VMEM((n, half, wide), f32),
            pltpu.VMEM((n, half, wide), bf16),
            pltpu.VMEM((n, half, wide), bf16),
            pltpu.VMEM((n, quarter, wide), f32),
            pltpu.VMEM((n, quarter, wide), bf16),
            pltpu.VMEM((n, quarter, wide), bf16),
            pltpu.VMEM((n, 4, quarter, joined), bf16),
            pltpu.VMEM((n, rows, cols), bf16),
            pltpu.VMEM((n, rows, cols), bf16),
            pltpu.VMEM((rows, cols), f32),
            dma((6,)),
            dma((2, n)),
            dma((n,)),
            dma((2 * n - 2,)),
            dma((n,)),
            dma((n,)),
            dma((n,)),
            dma((n,)),
            dma((n,)),
            dma((n, 3)),
            dma((n, 3)),
            dma((n,)),
            dma((n,)),
        ],
        compiler_params=pltpu.CompilerParams(
            collective_id=0, has_side_effects=True, vmem_limit_bytes=67043328
        ),
    )(expert_ids.T, gate_values.T, activations, expert_gate, expert_up, expert_down)


def shards(activations, expert_ids, gate_values, expert_gate, expert_up, expert_down):
    rows = activations.shape[0]
    experts_all = expert_gate.shape[0] * lax.axis_size("exp")
    capacity = 2 * rows * expert_ids.shape[1] // experts_all
    layer = dense_layer if capacity >= rows and lax.axis_size("tok") == 4 else slot_layer
    return layer(activations, expert_ids, gate_values, expert_gate, expert_up, expert_down)


def solution(mesh):
    placed = (
        P(("group", "exp"), "tok"),
        P(("group", "exp"), None),
        P(("group", "exp"), None),
        P("exp", "tok", None),
        P("exp", "tok", None),
        P("exp", None, "tok"),
    )
    return jax.shard_map(
        shards, mesh=mesh, in_specs=placed, out_specs=P(("group", "exp"), "tok"), check_vma=False
    )
```

```python
import functools

import jax
import jax.numpy as jnp
from jax import lax
from jax.experimental import pallas as pl
from jax.experimental.pallas import tpu as pltpu
from jax.sharding import PartitionSpec as P

MESH = pl.DeviceIdType.MESH


def slot_positions(expert_ids, experts_all, capacity):
    flat_ids = expert_ids.reshape(-1)
    one_hot = (flat_ids[:, None] == jnp.arange(experts_all, dtype=jnp.int32)[None, :]).astype(
        jnp.int32
    )
    earlier = jnp.cumsum(one_hot, axis=0) - one_hot
    rank_within = jnp.sum(earlier * one_hot, axis=1)
    return flat_ids * capacity + rank_within


def move_rows(buffer):
    return lax.all_to_all(buffer, "exp", split_axis=0, concat_axis=0, tiled=True)


def slot_layer(activations, expert_ids, gate_values, expert_gate, expert_up, expert_down):
    row_count, feature_cols = activations.shape
    top_count = expert_ids.shape[1]
    local_experts = expert_gate.shape[0]
    groups = lax.axis_size("exp")
    experts_all = local_experts * groups
    capacity = 2 * row_count * top_count // experts_all
    slot_index = slot_positions(expert_ids, experts_all, capacity)
    picked = jnp.repeat(activations, top_count, axis=0)
    outgoing = (
        jnp.zeros((experts_all * capacity, feature_cols), jnp.bfloat16).at[slot_index].set(picked)
    )
    arrived = move_rows(outgoing.reshape(groups, local_experts, capacity, feature_cols))
    gate_part = jnp.einsum(
        "sxcf,xfh->sxch", arrived, expert_gate, preferred_element_type=jnp.float32
    )
    up_part = jnp.einsum("sxcf,xfh->sxch", arrived, expert_up, preferred_element_type=jnp.float32)
    gate_pre, up_pre = (
        lax.psum(gate_part.astype(jnp.bfloat16), "tok").astype(jnp.float32),
        lax.psum(up_part.astype(jnp.bfloat16), "tok").astype(jnp.float32),
    )
    hidden = (jax.nn.silu(gate_pre) * up_pre).astype(jnp.bfloat16)
    results = jnp.einsum(
        "sxch,xhf->sxcf", hidden, expert_down, preferred_element_type=jnp.float32
    ).astype(jnp.bfloat16)
    returned = move_rows(results).reshape(experts_all * capacity, feature_cols)
    fetched = returned[slot_index].astype(jnp.float32).reshape(row_count, top_count, feature_cols)
    combined = jnp.sum(fetched * gate_values[:, :, None], axis=1)
    return combined.astype(jnp.bfloat16)


def block_order(n):
    return [sorted(range(n), key=lambda b: (abs(b - i), b)) for i in range(n)]


def run_order(n, pieces):
    m = n * pieces
    if n < 4 or pieces != 2:
        return [(k, s) for k in "FABCDE" for s in range(m) if s >= pieces or k not in "FA"]
    plan = [("F", 2), ("B", 0), ("F", 4), ("A", 2), ("F", 3), ("B", 1), ("F", 5)]
    for s in range(3, m - 2):
        plan += [("F", s)] if s > 5 else []
        plan += [("A", s), ("B", s - 1)]
    plan += [("F", m - 2), ("B", m - 3), ("F", m - 1)]
    plan += [("C", 2), ("A", m - 2), ("C", 3), ("A", m - 1), ("B", m - 2), ("C", 4), ("B", m - 1)]
    plan += [("C", s) for s in range(5, m - 2)]
    plan += [(k, s) for s in range(2, m - 4) for k in "DE"]
    for first, second in ((m - 2, m - 4), (m - 1, m - 3), (0, m - 2), (1, m - 1)):
        plan += [("C", first), ("D", second), ("E", second)]
    return plan + [(k, s) for s in range(2) for k in "DE"]


def dense_kernel(
    n, pieces, ids_hbm, gv_hbm, a_hbm, wg_hbm, wu_hbm, wd_hbm, out_ref,
    ids_ref, gv_ref, wg, wu, wd, gates, xg, keep, csend, crecv, mine, xsend, xrecv, hid, outb, ret, acc,
    w_sem, z_send, z_recv, g_send, g_recv, c_send, c_recv, x_send, x_recv, h_send, h_recv,
    r_send, r_recv,
):
    rows = xg.shape[1]
    local_experts, _, ff = wg.shape
    half, quarter = rows // 2, rows // 4
    me, t = lax.axis_index("exp"), lax.axis_index("tok")
    c, xx = lax.rem(t, 2), lax.div(t, 2)
    core_peer, chip_peer = {"tok": xx * 2 + 1 - c}, {"tok": (1 - xx) * 2 + c}
    own_q, chip_q = c * 2 + xx, c * 2 + 1 - xx
    table = block_order(n)

    def block(step):
        b = me * 0
        for i in range(n):
            b = jnp.where(me == i, table[i][step // pieces], b)
        return b

    def piece(step):
        return block(step) * pieces + step % pieces

    def send(src, dst, ss, rs, where):
        return pltpu.make_async_remote_copy(
            src_ref=src, dst_ref=dst, send_sem=ss, recv_sem=rs, device_id=where, device_id_type=MESH
        )

    loads = [
        pltpu.make_async_copy(src, dst, w_sem.at[slot])
        for slot, (src, dst) in enumerate(
            (
                *(
                    (a_hbm.at[pl.ds(i * rows, rows)], xg.at[me * pieces + i])
                    for i in range(pieces)
                ),
                (ids_hbm, ids_ref),
                (gv_hbm, gv_ref),
                (wg_hbm, wg),
                (wu_hbm, wu),
                (wd_hbm, wd),
            )
        )
    ]
    for copy in loads:
        copy.start()

    barrier = pltpu.get_barrier_semaphore()
    for j in range(1, n):
        pl.semaphore_signal(
            barrier, inc=1, device_id={"exp": lax.rem(me + j, n)}, device_id_type=MESH
        )
    for peer in (core_peer, chip_peer):
        pl.semaphore_signal(barrier, inc=1, device_id=peer, device_id_type=MESH)

    def spread(buffer, send_sem, recv_sem):
        return [
            (
                jnp.logical_and(peer >= 0, peer < n),
                send(
                    buffer.at[me], buffer.at[me], send_sem.at[i], recv_sem.at[me],
                    {"exp": jnp.clip(peer, 0, n - 1)},
                ),
            )
            for i, peer in enumerate(me + d * sign for d in range(1, n) for sign in (1, -1))
        ]

    gate_copies = spread(gates, g_send, g_recv)
    inner = jnp.logical_and(me > 0, me < n - 1)
    row_copies = [
        (
            jnp.logical_and(peer >= 0, peer < n),
            send(
                xg.at[me * pieces + h], xg.at[me * pieces + h],
                z_send.at[0, h * 2 + i], z_recv.at[me * pieces + h],
                {"exp": lax.rem(peer + n, n)},
            ),
        )
        for h in range(pieces)
        for i, peer in enumerate((me + 1, me - 1))
    ]

    def onward(s):
        b = block(s)
        peer, p = jnp.where(b < me, me + 1, me - 1), piece(s)
        return send(
            xg.at[p], xg.at[p], z_send.at[1, s], z_recv.at[p], {"exp": lax.rem(peer + n, n)}
        )

    def hand_rows(s):
        @pl.when(inner)
        def _():
            onward(s).wait_recv()
            onward(s).start()

    def to_core(s):
        return send(csend.at[s], crecv.at[s], c_send.at[s], c_recv.at[s], core_peer)

    def to_chip(s):
        return send(xsend.at[s], xrecv.at[s], x_send.at[s], x_recv.at[s], chip_peer)

    def hidden_copy(s, kind):
        q = (own_q, own_q, chip_q)[kind]
        peer = (chip_peer, core_peer, core_peer)[kind]
        return send(
            hid.at[s, q], hid.at[s, q], h_send.at[s, kind], h_recv.at[s, kind], peer
        )

    def hidden_arrival(s, kind):
        q = (chip_q, (1 - c) * 2 + xx, (1 - c) * 2 + 1 - xx)[kind]
        peer = (chip_peer, core_peer, core_peer)[kind]
        return send(
            hid.at[s, q], hid.at[s, q], h_send.at[s, kind], h_recv.at[s, kind], peer
        )

    def result_copy(s):
        b = block(s)
        p = me * pieces + s % pieces
        return send(outb.at[s], ret.at[p], r_send.at[s], r_recv.at[p], {"exp": b})

    def partial(s):
        b = piece(s)
        if s >= pieces:
            pl.when(jnp.logical_not(inner))(onward(s).wait_recv)
        first = pl.ds(pl.multiple_of(c * half, half), half)
        second = pl.ds(pl.multiple_of((1 - c) * half, half), half)
        block_rows = jnp.concatenate([xg[b, first, :], xg[b, second, :]], axis=0)
        for e in range(local_experts):
            for i, w in enumerate((wg, wu)):
                part = jnp.dot(block_rows, w[e], preferred_element_type=jnp.float32)
                cols = pl.ds((2 * e + i) * ff, ff)
                csend[s, :, cols] = part[half:].astype(jnp.bfloat16)
                keep[s, :, cols] = part[:half]
        to_core(s).start()

    def chip_sum(s):
        to_core(s).wait_recv()
        own = pl.ds(pl.multiple_of(xx * quarter, quarter), quarter)
        other = pl.ds(pl.multiple_of((1 - xx) * quarter, quarter), quarter)
        xsend[s] = (keep[s, other, :] + crecv[s, other, :].astype(jnp.float32)).astype(jnp.bfloat16)
        to_chip(s).start()
        mine[s] = keep[s, own, :] + crecv[s, own, :].astype(jnp.float32)

    def activate(s):
        b = block(s)
        if s >= pieces and s % pieces == 0:
            send(
                gates.at[b], gates.at[b], g_send.at[0], g_recv.at[b], {"exp": lax.rem(me + 1, n)}
            ).wait_recv()
        to_chip(s).wait_recv()
        square = (quarter, rows * pieces)
        diagonal = lax.broadcasted_iota(jnp.int32, square, 1) == (
            s % pieces * rows + own_q * quarter + lax.broadcasted_iota(jnp.int32, square, 0)
        )
        for e in range(local_experts):
            gate_cols, up_cols = pl.ds(2 * e * ff, ff), pl.ds((2 * e + 1) * ff, ff)
            g = mine[s, :, gate_cols] + xrecv[s, :, gate_cols].astype(jnp.float32)
            u = mine[s, :, up_cols] + xrecv[s, :, up_cols].astype(jnp.float32)
            weight_of = gates[b, pl.ds(me * local_experts + e, 1), :]
            scale = jnp.sum(jnp.where(diagonal, weight_of, 0.0), axis=1, keepdims=True)
            hid[s, own_q, :, pl.ds(e * ff, ff)] = (g / (1.0 + jnp.exp(-g)) * (u * scale)).astype(
                jnp.bfloat16
            )
        hidden_copy(s, 0).start()
        hidden_copy(s, 1).start()

    def hand_on(s):
        hidden_arrival(s, 0).wait_recv()
        hidden_copy(s, 2).start()

    def project(s):
        hidden_arrival(s, 1).wait_recv()
        hidden_arrival(s, 2).wait_recv()
        if s == first_projected:
            loads[-1].wait()
        h = hid[s].reshape(rows, local_experts * ff)
        result = jnp.dot(
            h, wd[...].reshape(local_experts * ff, wd.shape[2]), preferred_element_type=jnp.float32
        )
        if s < pieces:
            acc[s] = result
        else:
            outb[s] = result.astype(jnp.bfloat16)
            result_copy(s).start()

    stages = {"A": partial, "B": chip_sum, "C": activate, "D": hand_on, "E": project, "F": hand_rows}
    plan = run_order(n, pieces)
    first_projected = next(s for stage, s in plan if stage == "E")

    for copy in loads[: pieces + 2]:
        copy.wait()
    experts = lax.broadcasted_iota(jnp.int32, gates.shape[1:], 0)
    table_of_gates = jnp.zeros(gates.shape[1:], jnp.float32)
    for k in range(ids_ref.shape[0]):
        table_of_gates += jnp.where(experts == ids_ref[k : k + 1, :], gv_ref[k : k + 1, :], 0.0)
    gates[me] = table_of_gates
    pl.semaphore_wait(barrier, n + 1)
    for condition, copy in row_copies + gate_copies:
        pl.when(condition)(copy.start)
    for copy in loads[pieces + 2 : -1]:
        copy.wait()
    for h in range(pieces):
        partial(h)
    for stage, s in plan:
        stages[stage](s)

    for h in range(pieces):
        total = acc[h]
        for s in range(pieces + h, n * pieces, pieces):
            b, p = block(s), piece(s)
            send(outb.at[s], ret.at[p], r_send.at[s], r_recv.at[p], {"exp": b}).wait_recv()
            total += ret[p].astype(jnp.float32)
        out_ref[h * rows : (h + 1) * rows, :] = total.astype(out_ref.dtype)

    for s in range(n * pieces):
        to_core(s).wait_send()
        to_chip(s).wait_send()
        for kind in range(3):
            hidden_copy(s, kind).wait_send()
        if s >= pieces:
            result_copy(s).wait_send()
    for condition, copy in row_copies + gate_copies:
        pl.when(condition)(copy.wait_send)
    for s in range(pieces, n * pieces):
        pl.when(inner)(onward(s).wait_send)


def dense_layer(activations, expert_ids, gate_values, expert_gate, expert_up, expert_down):
    n = lax.axis_size("exp")
    rows, cols = activations.shape
    local_experts, _, ff = expert_gate.shape
    wide, joined = 2 * local_experts * ff, local_experts * ff
    pieces = 2 if rows % 128 == 0 else 1
    part = rows // pieces
    half, quarter, steps = part // 2, part // 4, n * pieces
    experts = -(-local_experts * n // 8) * 8
    top = expert_ids.shape[1]
    bf16, f32 = jnp.bfloat16, jnp.float32
    vmem, hbm = pl.BlockSpec(memory_space=pltpu.VMEM), pl.BlockSpec(memory_space=pltpu.HBM)
    dma = pltpu.SemaphoreType.DMA
    return pl.pallas_call(
        functools.partial(dense_kernel, n, pieces),
        out_shape=jax.ShapeDtypeStruct((rows, cols), bf16),
        in_specs=[hbm] * 6,
        out_specs=vmem,
        scratch_shapes=[
            pltpu.VMEM((top, rows), jnp.int32),
            pltpu.VMEM((top, rows), f32),
            pltpu.VMEM(expert_gate.shape, bf16),
            pltpu.VMEM(expert_up.shape, bf16),
            pltpu.VMEM(expert_down.shape, bf16),
            pltpu.VMEM((n, experts, rows), f32),
            pltpu.VMEM((steps, part, cols), bf16),
            pltpu.VMEM((steps, half, wide), f32),
            pltpu.VMEM((steps, half, wide), bf16),
            pltpu.VMEM((steps, half, wide), bf16),
            pltpu.VMEM((steps, quarter, wide), f32),
            pltpu.VMEM((steps, quarter, wide), bf16),
            pltpu.VMEM((steps, quarter, wide), bf16),
            pltpu.VMEM((steps, 4, quarter, joined), bf16),
            pltpu.VMEM((steps, part, cols), bf16),
            pltpu.VMEM((steps, part, cols), bf16),
            pltpu.VMEM((pieces, part, cols), f32),
            dma((5 + pieces,)),
            dma((2, steps)),
            dma((steps,)),
            dma((2 * n - 2,)),
            dma((steps,)),
            dma((steps,)),
            dma((steps,)),
            dma((steps,)),
            dma((steps,)),
            dma((steps, 3)),
            dma((steps, 3)),
            dma((steps,)),
            dma((steps,)),
        ],
        compiler_params=pltpu.CompilerParams(
            collective_id=0, has_side_effects=True, vmem_limit_bytes=67043328
        ),
    )(expert_ids.T, gate_values.T, activations, expert_gate, expert_up, expert_down)


def shards(activations, expert_ids, gate_values, expert_gate, expert_up, expert_down):
    rows = activations.shape[0]
    experts_all = expert_gate.shape[0] * lax.axis_size("exp")
    capacity = 2 * rows * expert_ids.shape[1] // experts_all
    layer = dense_layer if capacity >= rows and lax.axis_size("tok") == 4 else slot_layer
    return layer(activations, expert_ids, gate_values, expert_gate, expert_up, expert_down)


def solution(mesh):
    placed = (
        P(("group", "exp"), "tok"),
        P(("group", "exp"), None),
        P(("group", "exp"), None),
        P("exp", "tok", None),
        P("exp", "tok", None),
        P("exp", None, "tok"),
    )
    return jax.shard_map(
        shards, mesh=mesh, in_specs=placed, out_specs=P(("group", "exp"), "tok"), check_vma=False
    )
```

```python
import functools

import jax
import jax.numpy as jnp
from jax import lax
from jax.experimental import pallas as pl
from jax.experimental.pallas import tpu as pltpu
from jax.sharding import PartitionSpec as P

MESH = pl.DeviceIdType.MESH


def slot_positions(expert_ids, experts_all, capacity):
    flat_ids = expert_ids.reshape(-1)
    one_hot = (flat_ids[:, None] == jnp.arange(experts_all, dtype=jnp.int32)[None, :]).astype(
        jnp.int32
    )
    earlier = jnp.cumsum(one_hot, axis=0) - one_hot
    rank_within = jnp.sum(earlier * one_hot, axis=1)
    return flat_ids * capacity + rank_within


def move_rows(buffer):
    return lax.all_to_all(buffer, "exp", split_axis=0, concat_axis=0, tiled=True)


def slot_layer(activations, expert_ids, gate_values, expert_gate, expert_up, expert_down):
    row_count, feature_cols = activations.shape
    top_count = expert_ids.shape[1]
    local_experts = expert_gate.shape[0]
    groups = lax.axis_size("exp")
    experts_all = local_experts * groups
    capacity = 2 * row_count * top_count // experts_all
    slot_index = slot_positions(expert_ids, experts_all, capacity)
    picked = jnp.repeat(activations, top_count, axis=0)
    outgoing = (
        jnp.zeros((experts_all * capacity, feature_cols), jnp.bfloat16).at[slot_index].set(picked)
    )
    arrived = move_rows(outgoing.reshape(groups, local_experts, capacity, feature_cols))
    gate_part = jnp.einsum(
        "sxcf,xfh->sxch", arrived, expert_gate, preferred_element_type=jnp.float32
    )
    up_part = jnp.einsum("sxcf,xfh->sxch", arrived, expert_up, preferred_element_type=jnp.float32)
    gate_pre, up_pre = (
        lax.psum(gate_part.astype(jnp.bfloat16), "tok").astype(jnp.float32),
        lax.psum(up_part.astype(jnp.bfloat16), "tok").astype(jnp.float32),
    )
    hidden = (jax.nn.silu(gate_pre) * up_pre).astype(jnp.bfloat16)
    results = jnp.einsum(
        "sxch,xhf->sxcf", hidden, expert_down, preferred_element_type=jnp.float32
    ).astype(jnp.bfloat16)
    returned = move_rows(results).reshape(experts_all * capacity, feature_cols)
    fetched = returned[slot_index].astype(jnp.float32).reshape(row_count, top_count, feature_cols)
    combined = jnp.sum(fetched * gate_values[:, :, None], axis=1)
    return combined.astype(jnp.bfloat16)


def block_order(n):
    return [sorted(range(n), key=lambda b: (abs(b - i), b)) for i in range(n)]


def run_order(n, pieces):
    m = n * pieces
    if n < 4 or pieces != 2:
        return [(k, s) for k in "FABCDE" for s in range(m) if s >= pieces or k not in "FA"]
    plan = [("F", 2), ("B", 0), ("F", 4), ("A", 2), ("F", 3), ("B", 1), ("F", 5)]
    for s in range(3, m - 2):
        plan += [("F", s)] if s > 5 else []
        plan += [("A", s), ("B", s - 1)]
    plan += [("F", m - 2), ("B", m - 3), ("F", m - 1)]
    plan += [("C", 2), ("A", m - 2), ("C", 3), ("A", m - 1), ("B", m - 2), ("C", 4), ("B", m - 1)]
    plan += [("C", s) for s in range(5, m - 2)]
    plan += [(k, s) for s in range(2, m - 4) for k in "DE"]
    for first, second in ((m - 2, m - 4), (m - 1, m - 3), (0, m - 2), (1, m - 1)):
        plan += [("C", first), ("D", second), ("E", second)]
    return plan + [(k, s) for s in range(2) for k in "DE"]


def dense_kernel(
    n, pieces, ids_hbm, gv_hbm, a_hbm, wg_hbm, wu_hbm, wd_hbm, out_ref,
    ids_ref, gv_ref, wg, wu, wd, gates, xg, keep, csend, crecv, mine, xsend, xrecv, hid, outb, ret, acc,
    w_sem, z_send, z_recv, g_send, g_recv, c_send, c_recv, x_send, x_recv, h_send, h_recv,
    r_send, r_recv,
):
    rows = xg.shape[1]
    local_experts, _, ff = wg.shape
    half, quarter = rows // 2, rows // 4
    me, t = lax.axis_index("exp"), lax.axis_index("tok")
    c, xx = lax.rem(t, 2), lax.div(t, 2)
    core_peer, chip_peer = {"tok": xx * 2 + 1 - c}, {"tok": (1 - xx) * 2 + c}
    own_q, chip_q = c * 2 + xx, c * 2 + 1 - xx
    table = block_order(n)

    def block(step):
        b = me * 0
        for i in range(n):
            b = jnp.where(me == i, table[i][step // pieces], b)
        return b

    def piece(step):
        return block(step) * pieces + step % pieces

    def send(src, dst, ss, rs, where):
        return pltpu.make_async_remote_copy(
            src_ref=src, dst_ref=dst, send_sem=ss, recv_sem=rs, device_id=where, device_id_type=MESH
        )

    loads = [
        pltpu.make_async_copy(src, dst, w_sem.at[slot])
        for slot, (src, dst) in enumerate(
            (
                *(
                    (a_hbm.at[pl.ds(i * rows, rows)], xg.at[me * pieces + i])
                    for i in range(pieces)
                ),
                (ids_hbm, ids_ref),
                (gv_hbm, gv_ref),
                (wg_hbm, wg),
                (wu_hbm, wu),
                (wd_hbm, wd),
            )
        )
    ]
    barrier = pltpu.get_barrier_semaphore()
    for j in range(1, n):
        pl.semaphore_signal(
            barrier, inc=1, device_id={"exp": lax.rem(me + j, n)}, device_id_type=MESH
        )
    for peer in (core_peer, chip_peer):
        pl.semaphore_signal(barrier, inc=1, device_id=peer, device_id_type=MESH)

    for copy in loads:
        copy.start()

    def spread(buffer, send_sem, recv_sem):
        return [
            (
                jnp.logical_and(peer >= 0, peer < n),
                send(
                    buffer.at[me], buffer.at[me], send_sem.at[i], recv_sem.at[me],
                    {"exp": jnp.clip(peer, 0, n - 1)},
                ),
            )
            for i, peer in enumerate(me + d * sign for d in range(1, n) for sign in (1, -1))
        ]

    gate_copies = spread(gates, g_send, g_recv)
    inner = jnp.logical_and(me > 0, me < n - 1)
    row_copies = [
        (
            jnp.logical_and(peer >= 0, peer < n),
            send(
                xg.at[me * pieces + h], xg.at[me * pieces + h],
                z_send.at[0, h * 2 + i], z_recv.at[me * pieces + h],
                {"exp": lax.rem(peer + n, n)},
            ),
        )
        for h in range(pieces)
        for i, peer in enumerate((me + 1, me - 1))
    ]

    def onward(s):
        b = block(s)
        peer, p = jnp.where(b < me, me + 1, me - 1), piece(s)
        return send(
            xg.at[p], xg.at[p], z_send.at[1, s], z_recv.at[p], {"exp": lax.rem(peer + n, n)}
        )

    def hand_rows(s):
        @pl.when(inner)
        def _():
            onward(s).wait_recv()
            onward(s).start()

    def to_core(s):
        return send(csend.at[s], crecv.at[s], c_send.at[s], c_recv.at[s], core_peer)

    def to_chip(s):
        return send(xsend.at[s], xrecv.at[s], x_send.at[s], x_recv.at[s], chip_peer)

    def hidden_copy(s, kind):
        q = (own_q, own_q, chip_q)[kind]
        peer = (chip_peer, core_peer, core_peer)[kind]
        return send(
            hid.at[s, q], hid.at[s, q], h_send.at[s, kind], h_recv.at[s, kind], peer
        )

    def hidden_arrival(s, kind):
        q = (chip_q, (1 - c) * 2 + xx, (1 - c) * 2 + 1 - xx)[kind]
        peer = (chip_peer, core_peer, core_peer)[kind]
        return send(
            hid.at[s, q], hid.at[s, q], h_send.at[s, kind], h_recv.at[s, kind], peer
        )

    def result_copy(s):
        b = block(s)
        p = me * pieces + s % pieces
        return send(outb.at[s], ret.at[p], r_send.at[s], r_recv.at[p], {"exp": b})

    def partial(s):
        b = piece(s)
        if s >= pieces:
            pl.when(jnp.logical_not(inner))(onward(s).wait_recv)
        first = pl.ds(pl.multiple_of(c * half, half), half)
        second = pl.ds(pl.multiple_of((1 - c) * half, half), half)
        block_rows = jnp.concatenate([xg[b, first, :], xg[b, second, :]], axis=0)
        for e in range(local_experts):
            for i, w in enumerate((wg, wu)):
                part = jnp.dot(block_rows, w[e], preferred_element_type=jnp.float32)
                cols = pl.ds((2 * e + i) * ff, ff)
                csend[s, :, cols] = part[half:].astype(jnp.bfloat16)
                keep[s, :, cols] = part[:half]
        to_core(s).start()

    def chip_sum(s):
        to_core(s).wait_recv()
        own = pl.ds(pl.multiple_of(xx * quarter, quarter), quarter)
        other = pl.ds(pl.multiple_of((1 - xx) * quarter, quarter), quarter)
        xsend[s] = (keep[s, other, :] + crecv[s, other, :].astype(jnp.float32)).astype(jnp.bfloat16)
        to_chip(s).start()
        mine[s] = keep[s, own, :] + crecv[s, own, :].astype(jnp.float32)

    def activate(s):
        b = block(s)
        if s >= pieces and s % pieces == 0:
            send(
                gates.at[b], gates.at[b], g_send.at[0], g_recv.at[b], {"exp": lax.rem(me + 1, n)}
            ).wait_recv()
        to_chip(s).wait_recv()
        square = (quarter, rows * pieces)
        diagonal = lax.broadcasted_iota(jnp.int32, square, 1) == (
            s % pieces * rows + own_q * quarter + lax.broadcasted_iota(jnp.int32, square, 0)
        )
        for e in range(local_experts):
            gate_cols, up_cols = pl.ds(2 * e * ff, ff), pl.ds((2 * e + 1) * ff, ff)
            g = mine[s, :, gate_cols] + xrecv[s, :, gate_cols].astype(jnp.float32)
            u = mine[s, :, up_cols] + xrecv[s, :, up_cols].astype(jnp.float32)
            weight_of = gates[b, pl.ds(me * local_experts + e, 1), :]
            scale = jnp.sum(jnp.where(diagonal, weight_of, 0.0), axis=1, keepdims=True)
            hid[s, own_q, :, pl.ds(e * ff, ff)] = (g / (1.0 + jnp.exp(-g)) * (u * scale)).astype(
                jnp.bfloat16
            )
        hidden_copy(s, 0).start()
        hidden_copy(s, 1).start()

    def hand_on(s):
        hidden_arrival(s, 0).wait_recv()
        hidden_copy(s, 2).start()

    def project(s):
        hidden_arrival(s, 1).wait_recv()
        hidden_arrival(s, 2).wait_recv()
        if s == first_projected:
            loads[-1].wait()
        h = hid[s].reshape(rows, local_experts * ff)
        result = jnp.dot(
            h, wd[...].reshape(local_experts * ff, wd.shape[2]), preferred_element_type=jnp.float32
        )
        if s < pieces:
            acc[s] = result
        else:
            outb[s] = result.astype(jnp.bfloat16)
            result_copy(s).start()

    stages = {"A": partial, "B": chip_sum, "C": activate, "D": hand_on, "E": project, "F": hand_rows}
    plan = run_order(n, pieces)
    first_projected = next(s for stage, s in plan if stage == "E")

    for copy in loads[: pieces + 2]:
        copy.wait()
    experts = lax.broadcasted_iota(jnp.int32, gates.shape[1:], 0)
    table_of_gates = jnp.zeros(gates.shape[1:], jnp.float32)
    for k in range(ids_ref.shape[0]):
        table_of_gates += jnp.where(experts == ids_ref[k : k + 1, :], gv_ref[k : k + 1, :], 0.0)
    gates[me] = table_of_gates
    pl.semaphore_wait(barrier, n + 1)
    for condition, copy in row_copies + gate_copies:
        pl.when(condition)(copy.start)
    for copy in loads[pieces + 2 : -1]:
        copy.wait()
    for h in range(pieces):
        partial(h)
    for stage, s in plan:
        stages[stage](s)

    for h in range(pieces):
        total = acc[h]
        for s in range(pieces + h, n * pieces, pieces):
            b, p = block(s), piece(s)
            send(outb.at[s], ret.at[p], r_send.at[s], r_recv.at[p], {"exp": b}).wait_recv()
            total += ret[p].astype(jnp.float32)
        out_ref[h * rows : (h + 1) * rows, :] = total.astype(out_ref.dtype)

    for s in range(n * pieces):
        to_core(s).wait_send()
        to_chip(s).wait_send()
        for kind in range(3):
            hidden_copy(s, kind).wait_send()
        if s >= pieces:
            result_copy(s).wait_send()
    for condition, copy in row_copies + gate_copies:
        pl.when(condition)(copy.wait_send)
    for s in range(pieces, n * pieces):
        pl.when(inner)(onward(s).wait_send)


def dense_layer(activations, expert_ids, gate_values, expert_gate, expert_up, expert_down):
    n = lax.axis_size("exp")
    rows, cols = activations.shape
    local_experts, _, ff = expert_gate.shape
    wide, joined = 2 * local_experts * ff, local_experts * ff
    pieces = 2 if rows % 128 == 0 else 1
    part = rows // pieces
    half, quarter, steps = part // 2, part // 4, n * pieces
    experts = -(-local_experts * n // 8) * 8
    top = expert_ids.shape[1]
    bf16, f32 = jnp.bfloat16, jnp.float32
    vmem, hbm = pl.BlockSpec(memory_space=pltpu.VMEM), pl.BlockSpec(memory_space=pltpu.HBM)
    dma = pltpu.SemaphoreType.DMA
    return pl.pallas_call(
        functools.partial(dense_kernel, n, pieces),
        out_shape=jax.ShapeDtypeStruct((rows, cols), bf16),
        in_specs=[hbm] * 6,
        out_specs=vmem,
        scratch_shapes=[
            pltpu.VMEM((top, rows), jnp.int32),
            pltpu.VMEM((top, rows), f32),
            pltpu.VMEM(expert_gate.shape, bf16),
            pltpu.VMEM(expert_up.shape, bf16),
            pltpu.VMEM(expert_down.shape, bf16),
            pltpu.VMEM((n, experts, rows), f32),
            pltpu.VMEM((steps, part, cols), bf16),
            pltpu.VMEM((steps, half, wide), f32),
            pltpu.VMEM((steps, half, wide), bf16),
            pltpu.VMEM((steps, half, wide), bf16),
            pltpu.VMEM((steps, quarter, wide), f32),
            pltpu.VMEM((steps, quarter, wide), bf16),
            pltpu.VMEM((steps, quarter, wide), bf16),
            pltpu.VMEM((steps, 4, quarter, joined), bf16),
            pltpu.VMEM((steps, part, cols), bf16),
            pltpu.VMEM((steps, part, cols), bf16),
            pltpu.VMEM((pieces, part, cols), f32),
            dma((5 + pieces,)),
            dma((2, steps)),
            dma((steps,)),
            dma((2 * n - 2,)),
            dma((steps,)),
            dma((steps,)),
            dma((steps,)),
            dma((steps,)),
            dma((steps,)),
            dma((steps, 3)),
            dma((steps, 3)),
            dma((steps,)),
            dma((steps,)),
        ],
        compiler_params=pltpu.CompilerParams(
            collective_id=0, has_side_effects=True, vmem_limit_bytes=67043328
        ),
    )(expert_ids.T, gate_values.T, activations, expert_gate, expert_up, expert_down)


def shards(activations, expert_ids, gate_values, expert_gate, expert_up, expert_down):
    rows = activations.shape[0]
    experts_all = expert_gate.shape[0] * lax.axis_size("exp")
    capacity = 2 * rows * expert_ids.shape[1] // experts_all
    layer = dense_layer if capacity >= rows and lax.axis_size("tok") == 4 else slot_layer
    return layer(activations, expert_ids, gate_values, expert_gate, expert_up, expert_down)


def solution(mesh):
    placed = (
        P(("group", "exp"), "tok"),
        P(("group", "exp"), None),
        P(("group", "exp"), None),
        P("exp", "tok", None),
        P("exp", "tok", None),
        P("exp", None, "tok"),
    )
    return jax.shard_map(
        shards, mesh=mesh, in_specs=placed, out_specs=P(("group", "exp"), "tok"), check_vma=False
    )
```
